128 devices in a mesh: chan: 16 (over y, z), win: 8 (over x, core).
Axes of the slice: x: 4, y: 4, z: 4, core: 2. Of those that a mesh axis runs over, the one named last changes fastest.
Arguments:
- spectra: bfloat16 [768, 32, 2, 1024], P('chan', 'win'), may hold values from -120 to 120
- sources: int32 [4], replicated, may hold values from 0 to 767
- bin_rows: int32 [4, 16, 32, 3], P(None, 'chan'), may hold values from -1 to 47, as said below
Outputs:
- stacked: float32 [4, 32, 4096], P(None, 'chan', 'win')
The draws below stay inside these ranges and needn't reach their ends.
Inputs may be any that keep to these rules, and one draw needn't show every extreme that they name: `bin_rows`: for every step and every index d of chan, the entries name each of that device's 48 local receiver rows exactly once; within a bin the used slots come first and the rest are -1. In each step one bin uses all 3 slots on every device.
All inputs are finite; a program needn't handle non-finite values.
Results may differ from the reference program's by a relative error of at most 0.0099.
Values may be sent and summed in bfloat16 or wider, within the bound.
No kernel may reach another device: no remote copies, remote signals or barrier semaphores. Data moves between devices by JAX's collectives and lax.ppermute only.
A program may use at most 768 MiB of HBM per device.

```python
import math
import jax
import jax.numpy as jnp
from jax import lax

CH_DEV = 48
STEPS = 4
F = 1024
F0 = 32
NFFT = 8192
LMAX = 2048
HW = 32
NBINS = 32
MOST = 3
LAGS = 4096
CHANNELS = 768
WINDOWS = 32
N_CHAN = 16


def draw_spectra(key, part):
    first_key, second_key, third_key = jax.random.split(jax.random.fold_in(key, 5), 3)
    full_shape = (CHANNELS, WINDOWS, 2, F)
    base_noise = jnp.clip(jax.random.normal(first_key, full_shape, jnp.float32), -6.0, 6.0)
    channel_scale = jnp.exp(jax.random.uniform(second_key, (CHANNELS, WINDOWS, 1, 1), jnp.float32, 0.0, math.log(10.0)))
    band_scale = jnp.exp(jax.random.uniform(third_key, (CHANNELS, 1, 1, F), jnp.float32, math.log(0.5), math.log(2.0)))
    return (base_noise * channel_scale * band_scale).astype(jnp.bfloat16)


def draw_bin_rows(key, part):
    step_keys = jax.random.split(jax.random.fold_in(key, 11), STEPS)

    def one_step(step_key):
        weight_key, forced_key, device_key = jax.random.split(step_key, 3)
        weight = jax.random.randint(weight_key, (NBINS,), 0, 4)
        forced = jax.random.randint(forced_key, (), 0, NBINS)
        device_keys = jax.random.split(device_key, N_CHAN)

        def one_device(single_key):
            jitter_key, order_key = jax.random.split(single_key)
            jitter = jax.random.randint(jitter_key, (NBINS, MOST), 0, 1 << 14)
            bin_index = jnp.arange(NBINS, dtype=jnp.int32)
            scores = jitter + weight[:, None] * (1 << 12) + jnp.where(bin_index == forced, 1 << 16, 0)[:, None]
            flat_scores = scores.reshape(-1) * (NBINS * MOST) + jnp.arange(NBINS * MOST, dtype=jnp.int32)
            _, chosen = lax.top_k(flat_scores, CH_DEV)
            picked = jnp.zeros((NBINS * MOST,), jnp.int32).at[chosen].set(1).reshape(NBINS, MOST)
            counts = jnp.sum(picked, axis=1)
            filled = (jnp.arange(MOST, dtype=jnp.int32)[None, :] < counts[:, None]).astype(jnp.int32).reshape(-1)
            fill_rank = jnp.cumsum(filled) - 1
            row_order = jax.random.permutation(order_key, CH_DEV).astype(jnp.int32)
            entries = jnp.where(filled > 0, row_order[jnp.clip(fill_rank, 0, CH_DEV - 1)], -1)
            return entries.reshape(NBINS, MOST).astype(jnp.int32)
        return jax.vmap(one_device)(device_keys)
    return jax.vmap(one_step)(step_keys)


def touch_ends(values, own_key, smallest, largest):
    dims = values.shape
    index_at = [jax.random.randint(jax.random.fold_in(own_key, axis), (), 0, dims[axis]) for axis in range(len(dims))]
    values = values.at[tuple(index_at)].set(smallest)
    longest = dims.index(max(dims))
    index_at[longest] = (index_at[longest] + 1) % dims[longest]
    return values.at[tuple(index_at)].set(largest)


def setup_inputs(seed: int = 0) -> dict:
    keys = jax.random.split(jax.random.key(seed), 4)
    return {
        "spectra": draw_spectra(jax.random.fold_in(keys[3], 71), 0),
        "sources": touch_ends(jax.random.randint(keys[1], (STEPS,), 0, CHANNELS), jax.random.fold_in(keys[1], 1), 0, CHANNELS - 1).astype(jnp.int32),
        "bin_rows": draw_bin_rows(jax.random.fold_in(keys[3], 71), 0),
    }


epsilon_amp = 1e-06
phase_floor = 0.1

def band_matrix():
    index = jnp.arange(F, dtype=jnp.int32)
    inside = jnp.abs(index[:, None] - index[None, :]) <= HW
    return inside.astype(jnp.float32) / (2 * HW + 1)

def whiten(spectra):
    real_part = spectra[:, :, 0, :].astype(jnp.float32)
    imag_part = spectra[:, :, 1, :].astype(jnp.float32)
    amplitude = jnp.sqrt(real_part * real_part + imag_part * imag_part)
    smooth = jnp.dot(amplitude.reshape(-1, F), band_matrix(), precision=lax.Precision.HIGHEST)
    smooth = smooth.reshape(amplitude.shape) + epsilon_amp
    return jnp.stack([real_part / smooth, imag_part / smooth], axis=2).astype(jnp.bfloat16)

def cross_spectra(white, source):
    white_real = white[..., 0, :].astype(jnp.float32)
    white_imag = white[..., 1, :].astype(jnp.float32)
    source_real = source[..., 0, :].astype(jnp.float32)
    source_imag = source[..., 1, :].astype(jnp.float32)
    cross_real = white_real * source_real + white_imag * source_imag
    cross_imag = white_imag * source_real - white_real * source_imag
    return jnp.concatenate([cross_real, cross_imag], axis=-1).astype(jnp.bfloat16)

def lag_table(first_lag, lag_count):
    frequency = F0 + jnp.arange(F, dtype=jnp.int32)
    lag_index = first_lag + jnp.arange(lag_count, dtype=jnp.int32) - LMAX
    turn_count = jnp.mod(frequency[:, None] * lag_index[None, :], NFFT)
    angle_rad = turn_count.astype(jnp.float32) * (2.0 * jnp.pi / NFFT)
    cosine = jnp.cos(angle_rad)
    sine_part = jnp.sin(angle_rad)
    upper_half = jnp.concatenate([cosine, sine_part], axis=1)
    lower_half = jnp.concatenate([-sine_part, cosine], axis=1)
    return jnp.concatenate([upper_half, lower_half], axis=0).astype(jnp.bfloat16)

def correlate_block(cross_rows, first_lag, lag_count, windows):
    analytic = jnp.dot(cross_rows, lag_table(first_lag, lag_count), preferred_element_type=jnp.float32)
    analytic = analytic * (1.0 / jnp.sqrt(jnp.float32(F)))
    real_part = analytic[:, :lag_count]
    imag_part = analytic[:, lag_count:]
    magnitude = jnp.maximum(jnp.sqrt(real_part * real_part + imag_part * imag_part), phase_floor)
    terms = jnp.stack([real_part, real_part / magnitude, imag_part / magnitude], axis=1)
    return terms.reshape(-1, windows, 3, lag_count).sum(axis=1)

def weigh_stack(totals, counts, windows):
    traces = jnp.maximum(counts, 1.0) * windows
    linear = totals[..., 0, :]
    power = totals[..., 1, :] * totals[..., 1, :] + totals[..., 2, :] * totals[..., 2, :]
    return linear / jnp.sqrt(traces)[..., None] * power / traces[..., None]

def reference(spectra, sources, bin_rows):
    white = whiten(spectra)
    block_len = min(256, LAGS)
    block_count = LAGS // block_len
    device_base = jnp.arange(N_CHAN, dtype=jnp.int32)[:, None, None] * CH_DEV
    channel_index = jnp.arange(CHANNELS, dtype=jnp.int32)
    results = []
    for step_index in range(STEPS):
        source = lax.dynamic_index_in_dim(white, sources[step_index], 0, keepdims=False)
        cross_rows = cross_spectra(white, source).reshape(-1, 2 * F)
        slot_rows = bin_rows[step_index]
        is_live = slot_rows >= 0
        channel_ids = device_base + slot_rows
        member = lax.optimization_barrier(jnp.sum(((channel_ids[..., None] == channel_index) & is_live[..., None]).astype(jnp.float32), axis=(0, 2)))
        counts = lax.optimization_barrier(jnp.sum(member, axis=1))

        def one_block(block):
            partial_value = correlate_block(cross_rows, block * block_len, block_len, WINDOWS)
            return jnp.einsum('bc,ctl->btl', member, partial_value, precision=lax.Precision.HIGHEST)
        pieces = lax.map(one_block, jnp.arange(block_count, dtype=jnp.int32))
        totals = jnp.transpose(pieces, (1, 2, 0, 3)).reshape(NBINS, 3, LAGS)
        results.append(weigh_stack(totals, counts, WINDOWS))
    return jnp.stack(results)
```

```python
import jax
import jax.numpy as jnp
import numpy as np
from jax import lax
from jax.experimental import pallas as pl
from jax.experimental.pallas import tpu as pltpu
from jax.sharding import Mesh, PartitionSpec as P

F = 1024
F0 = 32
NFFT = 8192
HW = 32
NBINS = 32
EPS = 1e-06
FLOOR = 0.1
BLOCK = 512
HALF = 256
PAIRS = 4
bf16 = jnp.bfloat16
f32 = jnp.float32


def lag_tables():
    frequency = F0 + np.arange(F, dtype=np.int64)

    def pair(lags):
        angle = (frequency[:, None] * lags[None, :]) % NFFT * (2.0 * np.pi / NFFT)
        return np.concatenate([np.cos(angle), np.sin(angle)], axis=1).astype(bf16)

    blocks = [
        np.concatenate(
            [pair(b * BLOCK + h * HALF + np.arange(HALF)) for h in range(2)], axis=1
        )
        for b in range(PAIRS)
    ]
    return np.stack(blocks), pair(np.full((128,), 2048))


def smooth_amplitude(re, im):
    amp = jnp.sqrt(re * re + im * im)
    wide = F + 128
    padded = jnp.concatenate([amp, jnp.zeros((amp.shape[0], 128), f32)], axis=1)
    total = padded
    for k in (1, 2, 4, 8, 16, 32):
        total = total + pltpu.roll(total, k, 1)
    total = pltpu.roll(total, wide - HW, 1) + pltpu.roll(padded, HW, 1)
    return total[:, :F] * (1.0 / (2 * HW + 1)) + EPS


def whiten_kernel(x_ref, o_ref):
    for g in range(3):
        rows = slice(16 * g, 16 * g + 16)
        re = x_ref[0, 0, rows, :].astype(f32)
        im = x_ref[1, 0, rows, :].astype(f32)
        inv = 1.0 / smooth_amplitude(re, im)
        o_ref[0, 0, rows, :] = (re * inv).astype(bf16)
        o_ref[1, 0, rows, :] = (im * inv).astype(bf16)


def whiten(x):
    spec = pl.BlockSpec((2, 1, 48, F), lambda w: (0, w, 0, 0))
    return pl.pallas_call(
        whiten_kernel,
        grid=(x.shape[1],),
        in_specs=[spec],
        out_specs=spec,
        out_shape=jax.ShapeDtypeStruct(x.shape, bf16),
        name="whiten",
    )(x)


def stack_kernel(
    mine_ref, other_ref, src_ref, table_ref, edge_table_ref, member_ref, out_ref,
    src_sc, cross_sc, prod_sc, edge_prod_sc, minus_sc, edge_sc, sums_sc,
):
    step_id = pl.program_id(0)
    block = PAIRS - 1 - step_id
    floor2 = (FLOOR * 32.0) ** 2

    def unit(re, im):
        inv = lax.rsqrt(jnp.maximum(re * re + im * im, floor2))
        return re * inv, im * inv

    @pl.when(step_id == 0)
    def _():
        re = src_ref[0:16, :].astype(f32)
        im = src_ref[16:32, :].astype(f32)
        inv = 1.0 / smooth_amplitude(re, im)
        src_sc[0] = (re * inv).astype(bf16).astype(f32)
        src_sc[1] = (im * inv).astype(bf16).astype(f32)
        for s in range(2):
            for w in range(8):
                half, wl = divmod(w, 4)
                row = half * 8 + s * 4 + wl
                ref = other_ref if half else mine_ref
                for g in range(3):
                    rows = slice(16 * g, 16 * g + 16)
                    sr = jnp.broadcast_to(src_sc[0, row : row + 1, :], (16, F))
                    si = jnp.broadcast_to(src_sc[1, row : row + 1, :], (16, F))
                    wr = ref[0, wl, rows, :].astype(f32)
                    wi = ref[1, wl, rows, :].astype(f32)
                    at = w * 48 + 16 * g
                    cross_sc[s, at : at + 16, :] = (wr * sr + wi * si).astype(bf16)
                    cross_sc[s, 384 + at : 384 + at + 16, :] = (wi * sr - wr * si).astype(bf16)
        for s in range(2):
            edge_prod_sc[...] = jnp.dot(cross_sc[s], edge_table_ref[...], preferred_element_type=f32)
            for g in range(6):
                lin = jnp.zeros((8, 128), f32)
                pr, pi = lin, lin
                for w in range(8):
                    at = w * 48 + 8 * g
                    a = edge_prod_sc[at : at + 8, :128]
                    d = edge_prod_sc[at : at + 8, 128:]
                    c = edge_prod_sc[384 + at : 384 + at + 8, :128]
                    b = edge_prod_sc[384 + at : 384 + at + 8, 128:]
                    lin = lin + (a + b)
                    ur, ui = unit(a + b, c - d)
                    pr, pi = pr + ur, pi + ui
                for k, value in enumerate((lin, pr, pi)):
                    edge_sc[k, s, 8 * g : 8 * g + 8, :] = value

    def product(i):
        h, s = divmod(i, 2)
        prod_sc[i % 2] = jnp.dot(
            cross_sc[s], table_ref[0, :, h * 512 : h * 512 + 512], preferred_element_type=f32
        )

    def epilogue(i):
        h, s = divmod(i, 2)
        slot = i % 2
        for g in range(3):
            for t in range(2):
                zero = jnp.zeros((16, 128), f32)
                sa, sb, pr, pi, mr, mi = (zero,) * 6
                for w in range(8):
                    at = w * 48 + 16 * g
                    lo = slice(128 * t, 128 * t + 128)
                    hi = slice(256 + 128 * t, 256 + 128 * t + 128)
                    a = prod_sc[slot, at : at + 16, lo]
                    d = prod_sc[slot, at : at + 16, hi]
                    c = prod_sc[slot, 384 + at : 384 + at + 16, lo]
                    b = prod_sc[slot, 384 + at : 384 + at + 16, hi]
                    sa, sb = sa + a, sb + b
                    ur, ui = unit(a - b, c + d)
                    pr, pi = pr + ur, pi + ui
                    ur, ui = unit(a + b, c - d)
                    mr, mi = mr + ur, mi + ui
                at = h * 96 + s * 48 + 16 * g
                for k, value in enumerate((sa - sb, pr, pi)):
                    sums_sc[0, k, at : at + 16, 128 * t : 128 * t + 128] = value.astype(bf16)
                for k, value in enumerate((sa + sb, mr, mi)):
                    lo = 256 * h + 128 * t
                    minus_sc[k, s, 16 * g : 16 * g + 16, lo : lo + 128] = value

    product(0)
    for i in range(1, 4):
        product(i)
        epilogue(i - 1)
    epilogue(3)
    last = lax.broadcasted_iota(jnp.int32, (48, 128), 1) == 127
    for k in range(3):
        for s in range(2):
            moved = pltpu.roll(minus_sc[k, s], BLOCK - 1, 1)
            tail = moved[:, 384:]
            new_tail = jnp.where(last, edge_sc[k, s], tail)
            edge_sc[k, s] = tail
            at = s * 48
            sums_sc[1, k, at : at + 48, :] = moved[:, :256].astype(bf16)
            sums_sc[1, k, 96 + at : 96 + at + 48, :128] = moved[:, 256:384].astype(bf16)
            sums_sc[1, k, 96 + at : 96 + at + 48, 128:] = new_tail.astype(bf16)
    for sign in range(2):
        win = PAIRS - 1 - block if sign else PAIRS + block
        for k in range(3):
            binned = jnp.dot(member_ref[...], sums_sc[sign, k], preferred_element_type=f32)
            out_ref[:, win, k] = binned.reshape(16, 8, HALF).astype(bf16)


def stack_partial(mine, other, src, member):
    table, edge_table = lag_tables()
    whole = lambda *shape: pl.BlockSpec(shape, lambda b: (0,) * len(shape), pipeline_mode=pl.Buffered(1))
    return pl.pallas_call(
        stack_kernel,
        grid=(PAIRS,),
        in_specs=[
            whole(2, 4, 48, F),
            whole(2, 4, 48, F),
            whole(32, F),
            pl.BlockSpec((1, F, 1024), lambda b: (PAIRS - 1 - b, 0, 0)),
            whole(F, 256),
            whole(128, 192),
        ],
        out_specs=whole(16, 8, 3, 8, HALF),
        out_shape=jax.ShapeDtypeStruct((16, 8, 3, 8, HALF), bf16),
        scratch_shapes=[
            pltpu.VMEM((2, 16, F), f32),
            pltpu.VMEM((2, 768, F), bf16),
            pltpu.VMEM((2, 768, 512), f32),
            pltpu.VMEM((768, 256), f32),
            pltpu.VMEM((3, 2, 48, BLOCK), f32),
            pltpu.VMEM((3, 2, 48, 128), f32),
            pltpu.VMEM((2, 3, 192, HALF), bf16),
        ],
        compiler_params=pltpu.CompilerParams(vmem_limit_bytes=48 << 20),
        name="stack",
    )(mine, other, src, jnp.asarray(table), jnp.asarray(edge_table), member)


def shift(count):
    return [(i, (i + count) % 4) for i in range(4)]


def shards(spectra, sources, bin_rows):
    y, z, x, c = (lax.axis_index(a) for a in ("y", "z", "x", "c"))
    chan = y * 4 + z
    chan_dev, win_dev = spectra.shape[:2]
    windows = win_dev * 8
    swap = [(0, 1), (1, 0)]
    slot_rows = bin_rows[:, 0]

    owners, rows = sources // chan_dev, sources % chan_dev
    picked = [
        jnp.where(owners[s] == chan, lax.dynamic_index_in_dim(spectra, rows[s], 0, keepdims=False), 0)
        for s in range(4)
    ]
    counts = jnp.sum((slot_rows >= 0).astype(f32), axis=2).astype(bf16)
    counts = jnp.pad(counts.reshape(1, 128), ((0, 7), (0, F - 128)))
    sent = jnp.concatenate([jnp.stack(picked).reshape(32, F), counts], axis=0)
    for axis in ("z", "y"):
        got = [lax.ppermute(sent, axis, shift(k)) for k in (1, 3, 2)]
        sent = (sent + got[0]) + (got[1] + got[2])
    counts = sent[32, :128].astype(f32).reshape(4, NBINS)
    src = sent[:32].reshape(2, 2, 4, 2, F)
    src_mine = lax.dynamic_index_in_dim(src, c, 0, keepdims=False)
    src_other = lax.ppermute(lax.dynamic_index_in_dim(src, 1 - c, 0, keepdims=False), "c", swap)
    src = jnp.transpose(jnp.stack([src_mine, src_other]), (3, 0, 1, 2, 4)).reshape(32, F)

    mine = whiten(jnp.transpose(spectra, (2, 1, 0, 3)))
    other = lax.ppermute(mine, "c", swap)

    own_rows = lax.dynamic_slice_in_dim(slot_rows, 2 * c, 2, 0)
    member = jnp.any(own_rows[..., None] == jnp.arange(chan_dev), axis=2).reshape(2, 16, 2, chan_dev)
    member = jnp.transpose(member, (1, 0, 2, 3)).astype(bf16)
    eye = jnp.eye(2, dtype=bf16)
    member = (
        member[:, None, :, :, None, None, :]
        * eye[None, :, None, None, :, None, None]
        * eye[None, None, :, None, None, :, None]
    ).reshape(128, 4 * chan_dev)

    partial = stack_partial(mine, other, src, member)
    received = lax.all_to_all(partial.reshape(64, 6, 8, HALF), ("y", "z", "x"), 0, 0, tiled=True)
    totals = jnp.sum(received.astype(f32), axis=0).reshape(2, 3, 2, 2, 2, HALF)
    counts = lax.dynamic_slice(counts, (2 * c, 2 * chan), (2, 2))
    traces = (jnp.maximum(counts, 1.0) * windows)[None, None, :, :, None]
    linear, pr, pi = totals[:, 0] * (1.0 / 32.0), totals[:, 1], totals[:, 2]
    stacked = linear / jnp.sqrt(traces) * (pr * pr + pi * pi) / traces
    keep = lax.dynamic_index_in_dim(stacked, c, 0, keepdims=False)
    send = lax.dynamic_index_in_dim(stacked, 1 - c, 0, keepdims=False)
    got = lax.ppermute(send, "c", swap)
    both = jnp.where(c == 0, jnp.stack([keep, got]), jnp.stack([got, keep]))
    out = jnp.transpose(both, (0, 2, 3, 1, 4)).reshape(4, 2, BLOCK)
    return jnp.where(x < 2, out[..., ::-1], out)


def solution(mesh):
    fine = Mesh(mesh.devices.reshape(4, 4, 4, 2), ("y", "z", "x", "c"))
    chan, win = ("y", "z"), ("x", "c")
    in_specs = (P(chan, win, None, None), P(), P(None, chan, None, None))
    return jax.shard_map(
        shards, mesh=fine, in_specs=in_specs, out_specs=P(None, chan, win), check_vma=False
    )
```

```python
import jax
import jax.numpy as jnp
import numpy as np
from jax import lax
from jax.experimental import pallas as pl
from jax.experimental.pallas import tpu as pltpu
from jax.sharding import Mesh, PartitionSpec as P

F = 1024
F0 = 32
NFFT = 8192
HW = 32
NBINS = 32
EPS = 1e-06
FLOOR = 0.1
BLOCK = 512
HALF = 256
PAIRS = 4
bf16 = jnp.bfloat16
f32 = jnp.float32


def lag_tables():
    frequency = F0 + np.arange(F, dtype=np.int64)

    def pair(lags):
        angle = (frequency[:, None] * lags[None, :]) % NFFT * (2.0 * np.pi / NFFT)
        return np.concatenate([np.cos(angle), np.sin(angle)], axis=1).astype(bf16)

    blocks = [
        np.concatenate(
            [pair(b * BLOCK + h * HALF + np.arange(HALF)) for h in range(2)], axis=1
        )
        for b in range(PAIRS)
    ]
    return np.stack(blocks), pair(np.full((128,), 2048))


def smooth_amplitude(re, im):
    amp = jnp.sqrt(re * re + im * im)
    wide = F + 128
    padded = jnp.concatenate([amp, jnp.zeros((amp.shape[0], 128), f32)], axis=1)
    total = padded
    for k in (1, 2, 4, 8, 16, 32):
        total = total + pltpu.roll(total, k, 1)
    total = pltpu.roll(total, wide - HW, 1) + pltpu.roll(padded, HW, 1)
    return total[:, :F] * (1.0 / (2 * HW + 1)) + EPS


def pick_kernel(sources_ref, slots_ref, spectra_ref, out_ref, sem):
    me = lax.axis_index("y") * 4 + lax.axis_index("z")
    for s in range(4):
        owner, row = sources_ref[s] // 48, sources_ref[s] % 48
        copy = pltpu.make_async_copy(spectra_ref.at[row], out_ref.at[s], sem.at[s])

        @pl.when(owner == me)
        def _(copy=copy):
            copy.start()

        @pl.when(owner != me)
        def _(s=s):
            out_ref[s] = jnp.zeros((4, 2, F), bf16)

    out_ref[4] = jnp.zeros((4, 2, F), bf16)
    for s in range(4):
        live = (slots_ref[s] >= 0).astype(f32)
        count = live[0] + live[1] + live[2]
        out_ref[4, s, :, :NBINS] = jnp.broadcast_to(count, (2, NBINS)).astype(bf16)
    for s in range(4):
        owner, row = sources_ref[s] // 48, sources_ref[s] % 48
        copy = pltpu.make_async_copy(spectra_ref.at[row], out_ref.at[s], sem.at[s])

        @pl.when(owner == me)
        def _(copy=copy):
            copy.wait()


def pick(spectra, sources, slots):
    return pl.pallas_call(
        pick_kernel,
        in_specs=[
            pl.BlockSpec(memory_space=pltpu.SMEM),
            pl.BlockSpec(memory_space=pltpu.VMEM),
            pl.BlockSpec(memory_space=pl.ANY),
        ],
        out_specs=pl.BlockSpec(memory_space=pltpu.VMEM),
        out_shape=jax.ShapeDtypeStruct((5, 4, 2, F), bf16),
        scratch_shapes=[pltpu.SemaphoreType.DMA((4,))],
        name="pick",
    )(sources, slots, spectra)


def whiten_kernel(x_ref, o_ref):
    for g in range(3):
        rows = slice(16 * g, 16 * g + 16)
        re = x_ref[0, 0, rows, :].astype(f32)
        im = x_ref[1, 0, rows, :].astype(f32)
        inv = 1.0 / smooth_amplitude(re, im)
        o_ref[0, 0, rows, :] = (re * inv).astype(bf16)
        o_ref[1, 0, rows, :] = (im * inv).astype(bf16)


def whiten(x):
    spec = pl.BlockSpec((2, 1, 48, F), lambda w: (0, w, 0, 0))
    return pl.pallas_call(
        whiten_kernel,
        grid=(x.shape[1],),
        in_specs=[spec],
        out_specs=spec,
        out_shape=jax.ShapeDtypeStruct(x.shape, bf16),
        name="whiten",
    )(x)


def stack_kernel(
    part0_ref, part1_ref, part2_ref, part3_ref, src_ref, table_ref, edge_table_ref, member_ref, out_ref,
    src_sc, cross_sc, prod_sc, edge_prod_sc, minus_sc, edge_sc, sums_sc,
):
    step_id = pl.program_id(0)
    block = PAIRS - 1 - step_id
    floor2 = (FLOOR * 32.0) ** 2

    def unit(re, im):
        inv = lax.rsqrt(jnp.maximum(re * re + im * im, floor2))
        return re * inv, im * inv

    @pl.when(step_id == 0)
    def _():
        re = src_ref[0:16, :].astype(f32)
        im = src_ref[16:32, :].astype(f32)
        inv = 1.0 / smooth_amplitude(re, im)
        src_sc[0] = (re * inv).astype(bf16).astype(f32)
        src_sc[1] = (im * inv).astype(bf16).astype(f32)
        for s in range(2):
            for w in range(8):
                half, wl = divmod(w, 4)
                row = half * 8 + s * 4 + wl
                ref = (part0_ref, part1_ref, part2_ref, part3_ref)[w // 2]
                for g in range(3):
                    rows = slice(16 * g, 16 * g + 16)
                    sr = jnp.broadcast_to(src_sc[0, row : row + 1, :], (16, F))
                    si = jnp.broadcast_to(src_sc[1, row : row + 1, :], (16, F))
                    wr = ref[0, w % 2, rows, :].astype(f32)
                    wi = ref[1, w % 2, rows, :].astype(f32)
                    at = w * 48 + 16 * g
                    cross_sc[s, at : at + 16, :] = (wr * sr + wi * si).astype(bf16)
                    cross_sc[s, 384 + at : 384 + at + 16, :] = (wi * sr - wr * si).astype(bf16)
        for s in range(2):
            edge_prod_sc[...] = jnp.dot(cross_sc[s], edge_table_ref[...], preferred_element_type=f32)
            for g in range(6):
                lin = jnp.zeros((8, 128), f32)
                pr, pi = lin, lin
                for w in range(8):
                    at = w * 48 + 8 * g
                    a = edge_prod_sc[at : at + 8, :128]
                    d = edge_prod_sc[at : at + 8, 128:]
                    c = edge_prod_sc[384 + at : 384 + at + 8, :128]
                    b = edge_prod_sc[384 + at : 384 + at + 8, 128:]
                    lin = lin + (a + b)
                    ur, ui = unit(a + b, c - d)
                    pr, pi = pr + ur, pi + ui
                for k, value in enumerate((lin, pr, pi)):
                    edge_sc[k, s, 8 * g : 8 * g + 8, :] = value

    def product(i):
        h, s = divmod(i, 2)
        prod_sc[i % 2] = jnp.dot(
            cross_sc[s], table_ref[0, :, h * 512 : h * 512 + 512], preferred_element_type=f32
        )

    def epilogue(i):
        h, s = divmod(i, 2)
        slot = i % 2
        for g in range(3):
            for t in range(2):
                zero = jnp.zeros((16, 128), f32)
                sa, sb, pr, pi, mr, mi = (zero,) * 6
                for w in range(8):
                    at = w * 48 + 16 * g
                    lo = slice(128 * t, 128 * t + 128)
                    hi = slice(256 + 128 * t, 256 + 128 * t + 128)
                    a = prod_sc[slot, at : at + 16, lo]
                    d = prod_sc[slot, at : at + 16, hi]
                    c = prod_sc[slot, 384 + at : 384 + at + 16, lo]
                    b = prod_sc[slot, 384 + at : 384 + at + 16, hi]
                    sa, sb = sa + a, sb + b
                    ur, ui = unit(a - b, c + d)
                    pr, pi = pr + ur, pi + ui
                    ur, ui = unit(a + b, c - d)
                    mr, mi = mr + ur, mi + ui
                at = h * 96 + s * 48 + 16 * g
                for k, value in enumerate((sa - sb, pr, pi)):
                    sums_sc[0, k, at : at + 16, 128 * t : 128 * t + 128] = value.astype(bf16)
                for k, value in enumerate((sa + sb, mr, mi)):
                    lo = 256 * h + 128 * t
                    minus_sc[k, s, 16 * g : 16 * g + 16, lo : lo + 128] = value

    product(0)
    for i in range(1, 4):
        product(i)
        epilogue(i - 1)
    epilogue(3)
    last = lax.broadcasted_iota(jnp.int32, (48, 128), 1) == 127
    for k in range(3):
        for s in range(2):
            moved = pltpu.roll(minus_sc[k, s], BLOCK - 1, 1)
            tail = moved[:, 384:]
            new_tail = jnp.where(last, edge_sc[k, s], tail)
            edge_sc[k, s] = tail
            at = s * 48
            sums_sc[1, k, at : at + 48, :] = moved[:, :256].astype(bf16)
            sums_sc[1, k, 96 + at : 96 + at + 48, :128] = moved[:, 256:384].astype(bf16)
            sums_sc[1, k, 96 + at : 96 + at + 48, 128:] = new_tail.astype(bf16)
    for sign in range(2):
        win = PAIRS - 1 - block if sign else PAIRS + block
        for k in range(3):
            binned = jnp.dot(member_ref[...], sums_sc[sign, k], preferred_element_type=f32)
            out_ref[:, win, k] = binned.reshape(16, 8, HALF).astype(bf16)


def stack_partial(parts, src, member):
    table, edge_table = lag_tables()
    whole = lambda *shape: pl.BlockSpec(shape, lambda b: (0,) * len(shape), pipeline_mode=pl.Buffered(1))
    return pl.pallas_call(
        stack_kernel,
        grid=(PAIRS,),
        in_specs=[
            *[whole(2, 2, 48, F)] * 4,
            whole(32, F),
            pl.BlockSpec((1, F, 1024), lambda b: (PAIRS - 1 - b, 0, 0)),
            whole(F, 256),
            whole(128, 192),
        ],
        out_specs=whole(16, 8, 3, 8, HALF),
        out_shape=jax.ShapeDtypeStruct((16, 8, 3, 8, HALF), bf16),
        scratch_shapes=[
            pltpu.VMEM((2, 16, F), f32),
            pltpu.VMEM((2, 768, F), bf16),
            pltpu.VMEM((2, 768, 512), f32),
            pltpu.VMEM((768, 256), f32),
            pltpu.VMEM((3, 2, 48, BLOCK), f32),
            pltpu.VMEM((3, 2, 48, 128), f32),
            pltpu.VMEM((2, 3, 192, HALF), bf16),
        ],
        compiler_params=pltpu.CompilerParams(vmem_limit_bytes=48 << 20),
        name="stack",
    )(*parts, src, jnp.asarray(table), jnp.asarray(edge_table), member)


def shift(count):
    return [(i, (i + count) % 4) for i in range(4)]


def shards(spectra, sources, bin_rows):
    y, z, x, c = (lax.axis_index(a) for a in ("y", "z", "x", "c"))
    chan = y * 4 + z
    chan_dev, win_dev = spectra.shape[:2]
    windows = win_dev * 8
    swap = [(0, 1), (1, 0)]
    slot_rows = bin_rows[:, 0]

    sent = pick(spectra, sources, jnp.transpose(bin_rows, (0, 3, 1, 2)))
    flipped = jnp.transpose(spectra, (2, 1, 0, 3))
    early, late = whiten(flipped[:, :2]), flipped[:, 2:]
    for axis in ("z", "y"):
        got = [lax.ppermute(sent, axis, shift(k)) for k in (1, 3, 2)]
        sent = (sent + got[0]) + (got[1] + got[2])
        if axis == "z":
            sent, late = lax.optimization_barrier((sent, late))
            late = whiten(late)
    counts = sent[4, :, 0, :NBINS].astype(f32)
    src = sent[:4].reshape(2, 2, 4, 2, F)
    src_mine = lax.dynamic_index_in_dim(src, c, 0, keepdims=False)
    src_other = lax.ppermute(lax.dynamic_index_in_dim(src, 1 - c, 0, keepdims=False), "c", swap)
    src = jnp.transpose(jnp.stack([src_mine, src_other]), (3, 0, 1, 2, 4)).reshape(32, F)
    parts = [early, late, lax.ppermute(early, "c", swap), lax.ppermute(late, "c", swap)]

    own_rows = lax.dynamic_slice_in_dim(slot_rows, 2 * c, 2, 0)
    member = jnp.any(own_rows[..., None] == jnp.arange(chan_dev), axis=2).reshape(2, 16, 2, chan_dev)
    member = jnp.transpose(member, (1, 0, 2, 3)).astype(bf16)
    eye = jnp.eye(2, dtype=bf16)
    member = (
        member[:, None, :, :, None, None, :]
        * eye[None, :, None, None, :, None, None]
        * eye[None, None, :, None, None, :, None]
    ).reshape(128, 4 * chan_dev)

    partial = stack_partial(parts, src, member)
    received = lax.all_to_all(partial.reshape(64, 6, 8, HALF), ("y", "z", "x"), 0, 0, tiled=True)
    totals = jnp.sum(received.astype(f32), axis=0).reshape(2, 3, 2, 2, 2, HALF)
    counts = lax.dynamic_slice(counts, (2 * c, 2 * chan), (2, 2))
    traces = (jnp.maximum(counts, 1.0) * windows)[None, None, :, :, None]
    linear, pr, pi = totals[:, 0] * (1.0 / 32.0), totals[:, 1], totals[:, 2]
    stacked = linear / jnp.sqrt(traces) * (pr * pr + pi * pi) / traces
    keep = lax.dynamic_index_in_dim(stacked, c, 0, keepdims=False)
    send = lax.dynamic_index_in_dim(stacked, 1 - c, 0, keepdims=False)
    got = lax.ppermute(send, "c", swap)
    both = jnp.where(c == 0, jnp.stack([keep, got]), jnp.stack([got, keep]))
    out = jnp.transpose(both, (0, 2, 3, 1, 4)).reshape(4, 2, BLOCK)
    return jnp.where(x < 2, out[..., ::-1], out)


def solution(mesh):
    fine = Mesh(mesh.devices.reshape(4, 4, 4, 2), ("y", "z", "x", "c"))
    chan, win = ("y", "z"), ("x", "c")
    in_specs = (P(chan, win, None, None), P(), P(None, chan, None, None))
    return jax.shard_map(
        shards, mesh=fine, in_specs=in_specs, out_specs=P(None, chan, win), check_vma=False
    )
```

```python
import jax
import jax.numpy as jnp
import numpy as np
from jax import lax
from jax.experimental import pallas as pl
from jax.experimental.pallas import tpu as pltpu
from jax.sharding import Mesh, PartitionSpec as P

F = 1024
F0 = 32
NFFT = 8192
HW = 32
NBINS = 32
EPS = 1e-06
FLOOR = 0.1
BLOCK = 512
HALF = 256
PAIRS = 4
bf16 = jnp.bfloat16
f32 = jnp.float32


def lag_tables():
    frequency = F0 + np.arange(F, dtype=np.int64)

    def pair(lags):
        angle = (frequency[:, None] * lags[None, :]) % NFFT * (2.0 * np.pi / NFFT)
        return np.concatenate([np.cos(angle), np.sin(angle)], axis=1).astype(bf16)

    blocks = [
        np.concatenate(
            [pair(b * BLOCK + h * HALF + np.arange(HALF)) for h in range(2)], axis=1
        )
        for b in range(PAIRS)
    ]
    return np.stack(blocks), pair(np.full((128,), 2048))


def smooth_amplitude(re, im):
    amp = jnp.sqrt(re * re + im * im)
    wide = F + 128
    padded = jnp.concatenate([amp, jnp.zeros((amp.shape[0], 128), f32)], axis=1)
    total = padded
    for k in (1, 2, 4, 8, 16, 32):
        total = total + pltpu.roll(total, k, 1)
    total = pltpu.roll(total, wide - HW, 1) + pltpu.roll(padded, HW, 1)
    return total[:, :F] * (1.0 / (2 * HW + 1)) + EPS


def pick_kernel(sources_ref, slots_ref, spectra_ref, out_ref, sem):
    me = lax.axis_index("y") * 4 + lax.axis_index("z")
    for s in range(4):
        owner, row = sources_ref[s] // 48, sources_ref[s] % 48
        copy = pltpu.make_async_copy(spectra_ref.at[row], out_ref.at[s, :, :, pl.ds(0, F)], sem.at[s])

        @pl.when(owner == me)
        def _(copy=copy):
            copy.start()

        @pl.when(owner != me)
        def _(s=s):
            out_ref[s, :, :, :F] = jnp.zeros((4, 2, F), bf16)

        live = (slots_ref[s] >= 0).astype(f32)
        count = live[0] + live[1] + live[2]
        out_ref[s, :, :, F:] = jnp.zeros((4, 2, 128), bf16)
        out_ref[s, 0, :, F : F + NBINS] = jnp.broadcast_to(count, (2, NBINS)).astype(bf16)

    for s in range(4):
        owner, row = sources_ref[s] // 48, sources_ref[s] % 48
        copy = pltpu.make_async_copy(spectra_ref.at[row], out_ref.at[s, :, :, pl.ds(0, F)], sem.at[s])

        @pl.when(owner == me)
        def _(copy=copy):
            copy.wait()


def pick(spectra, sources, slots):
    return pl.pallas_call(
        pick_kernel,
        in_specs=[
            pl.BlockSpec(memory_space=pltpu.SMEM),
            pl.BlockSpec(memory_space=pltpu.VMEM),
            pl.BlockSpec(memory_space=pl.ANY),
        ],
        out_specs=pl.BlockSpec(memory_space=pltpu.VMEM),
        out_shape=jax.ShapeDtypeStruct((4, 4, 2, F + 128), bf16),
        scratch_shapes=[pltpu.SemaphoreType.DMA((4,))],
        name="pick",
    )(sources, slots, spectra)


def whiten_kernel(x_ref, band_ref, o_ref, amp_sc):
    edge = jnp.zeros((384, 128), bf16)
    amp_sc[:, :128] = edge
    amp_sc[:, 128 + F :] = edge
    for w in range(4):
        re = x_ref[0, w].astype(f32)
        im = x_ref[1, w].astype(f32)
        amp = jnp.sqrt(re * re + im * im)
        high = amp.astype(bf16)
        amp_sc[48 * w : 48 * w + 48, 128 : 128 + F] = high
        amp_sc[192 + 48 * w : 192 + 48 * w + 48, 128 : 128 + F] = (amp - high.astype(f32)).astype(bf16)
    for n in range(4):
        lanes = slice(256 * n, 256 * n + 256)
        total = jnp.dot(amp_sc[:, 256 * n : 256 * n + 512], band_ref[...], preferred_element_type=f32)
        total = (total[:192] + total[192:]) * (1.0 / (2 * HW + 1)) + EPS
        inv = 1.0 / total
        for w in range(4):
            part = inv[48 * w : 48 * w + 48]
            o_ref[0, w, :, lanes] = (x_ref[0, w, :, lanes].astype(f32) * part).astype(bf16)
            o_ref[1, w, :, lanes] = (x_ref[1, w, :, lanes].astype(f32) * part).astype(bf16)


def whiten(x, band):
    vmem = pl.BlockSpec(memory_space=pltpu.VMEM)
    return pl.pallas_call(
        whiten_kernel,
        in_specs=[vmem, vmem],
        out_specs=vmem,
        out_shape=jax.ShapeDtypeStruct(x.shape, bf16),
        scratch_shapes=[pltpu.VMEM((384, F + 256), bf16)],
        cost_estimate=pl.CostEstimate(flops=8 * 10**8, bytes_accessed=2 * 10**6, transcendentals=4 * 10**5),
        name="whiten",
    )(x, band)


def stack_kernel(
    mine_ref, other_ref, src_ref, table_ref, edge_table_ref, member_ref, out_ref,
    src_sc, cross_sc, prod_sc, edge_prod_sc, minus_sc, edge_sc, sums_sc, table_sc, table_sem, part_sc, part_sem,
):
    step_id = pl.program_id(0)
    block = PAIRS - 1 - step_id
    floor2 = (FLOOR * 32.0) ** 2
    slot = step_id % 2

    def fetch(step):
        return pltpu.make_async_copy(table_ref.at[PAIRS - 1 - step], table_sc.at[step % 2], table_sem.at[step % 2])

    parts = [
        pltpu.make_async_copy(ref, part_sc.at[i], part_sem.at[i])
        for i, ref in enumerate((mine_ref, other_ref))
    ]

    @pl.when(step_id == 0)
    def _():
        for copy in parts:
            copy.start()
        fetch(0).start()

    @pl.when(step_id < PAIRS - 1)
    def _():
        fetch(step_id + 1).start()

    def unit(re, im):
        inv = lax.rsqrt(jnp.maximum(re * re + im * im, floor2))
        return re * inv, im * inv

    @pl.when(step_id == 0)
    def _():
        re = src_ref[0:16, :].astype(f32)
        im = src_ref[16:32, :].astype(f32)
        inv = 1.0 / smooth_amplitude(re, im)
        src_sc[0] = (re * inv).astype(bf16).astype(f32)
        src_sc[1] = (im * inv).astype(bf16).astype(f32)
        for w in range(8):
            half, wl = divmod(w, 4)
            if wl == 0:
                parts[half].wait()
            for s in range(2):
                row = half * 8 + s * 4 + wl
                ref = part_sc.at[half]
                for g in range(3):
                    rows = slice(16 * g, 16 * g + 16)
                    sr = jnp.broadcast_to(src_sc[0, row : row + 1, :], (16, F))
                    si = jnp.broadcast_to(src_sc[1, row : row + 1, :], (16, F))
                    wr = ref[0, wl, rows, :].astype(f32)
                    wi = ref[1, wl, rows, :].astype(f32)
                    at = w * 48 + 16 * g
                    cross_sc[s, at : at + 16, :] = (wr * sr + wi * si).astype(bf16)
                    cross_sc[s, 384 + at : 384 + at + 16, :] = (wi * sr - wr * si).astype(bf16)
        for s in range(2):
            edge_prod_sc[...] = jnp.dot(cross_sc[s], edge_table_ref[...], preferred_element_type=f32)
            for g in range(6):
                lin = jnp.zeros((8, 128), f32)
                pr, pi = lin, lin
                for w in range(8):
                    at = w * 48 + 8 * g
                    a = edge_prod_sc[at : at + 8, :128]
                    d = edge_prod_sc[at : at + 8, 128:]
                    c = edge_prod_sc[384 + at : 384 + at + 8, :128]
                    b = edge_prod_sc[384 + at : 384 + at + 8, 128:]
                    lin = lin + (a + b)
                    ur, ui = unit(a + b, c - d)
                    pr, pi = pr + ur, pi + ui
                for k, value in enumerate((lin, pr, pi)):
                    edge_sc[k, s, 8 * g : 8 * g + 8, :] = value

    def product(i):
        h, s = divmod(i, 2)
        prod_sc[i % 2] = jnp.dot(
            cross_sc[s], table_sc[slot, :, h * 512 : h * 512 + 512], preferred_element_type=f32
        )

    def epilogue(i):
        h, s = divmod(i, 2)
        slot = i % 2
        for g in range(3):
            for t in range(2):
                zero = jnp.zeros((16, 128), f32)
                sa, sb, pr, pi, mr, mi = (zero,) * 6
                for w in range(8):
                    at = w * 48 + 16 * g
                    lo = slice(128 * t, 128 * t + 128)
                    hi = slice(256 + 128 * t, 256 + 128 * t + 128)
                    a = prod_sc[slot, at : at + 16, lo]
                    d = prod_sc[slot, at : at + 16, hi]
                    c = prod_sc[slot, 384 + at : 384 + at + 16, lo]
                    b = prod_sc[slot, 384 + at : 384 + at + 16, hi]
                    sa, sb = sa + a, sb + b
                    ur, ui = unit(a - b, c + d)
                    pr, pi = pr + ur, pi + ui
                    ur, ui = unit(a + b, c - d)
                    mr, mi = mr + ur, mi + ui
                at = h * 96 + s * 48 + 16 * g
                for k, value in enumerate((sa - sb, pr, pi)):
                    sums_sc[0, k, at : at + 16, 128 * t : 128 * t + 128] = value.astype(bf16)
                for k, value in enumerate((sa + sb, mr, mi)):
                    lo = 256 * h + 128 * t
                    minus_sc[k, s, 16 * g : 16 * g + 16, lo : lo + 128] = value

    fetch(step_id).wait()
    product(0)
    for i in range(1, 4):
        product(i)
        epilogue(i - 1)
    epilogue(3)
    last = lax.broadcasted_iota(jnp.int32, (48, 128), 1) == 127
    for k in range(3):
        for s in range(2):
            moved = pltpu.roll(minus_sc[k, s], BLOCK - 1, 1)
            tail = moved[:, 384:]
            new_tail = jnp.where(last, edge_sc[k, s], tail)
            edge_sc[k, s] = tail
            at = s * 48
            sums_sc[1, k, at : at + 48, :] = moved[:, :256].astype(bf16)
            sums_sc[1, k, 96 + at : 96 + at + 48, :128] = moved[:, 256:384].astype(bf16)
            sums_sc[1, k, 96 + at : 96 + at + 48, 128:] = new_tail.astype(bf16)
    for sign in range(2):
        win = PAIRS - 1 - block if sign else PAIRS + block
        for k in range(3):
            binned = jnp.dot(member_ref[...], sums_sc[sign, k], preferred_element_type=f32)
            out_ref[:, win, k] = binned.reshape(16, 8, HALF).astype(bf16)


def stack_partial(parts, src, member):
    table, edge_table = lag_tables()
    hbm = pl.BlockSpec(memory_space=pl.ANY)
    vmem = pl.BlockSpec(memory_space=pltpu.VMEM)
    return pl.pallas_call(
        stack_kernel,
        grid=(PAIRS,),
        in_specs=[hbm, hbm, vmem, hbm, vmem, vmem],
        out_specs=vmem,
        out_shape=jax.ShapeDtypeStruct((16, 8, 3, 8, HALF), bf16),
        scratch_shapes=[
            pltpu.VMEM((2, 16, F), f32),
            pltpu.VMEM((2, 768, F), bf16),
            pltpu.VMEM((2, 768, 512), f32),
            pltpu.VMEM((768, 256), f32),
            pltpu.VMEM((3, 2, 48, BLOCK), f32),
            pltpu.VMEM((3, 2, 48, 128), f32),
            pltpu.VMEM((2, 3, 192, HALF), bf16),
            pltpu.VMEM((2, F, 1024), bf16),
            pltpu.SemaphoreType.DMA((2,)),
            pltpu.VMEM((2, 2, 4, 48, F), bf16),
            pltpu.SemaphoreType.DMA((2,)),
        ],
        compiler_params=pltpu.CompilerParams(vmem_limit_bytes=48 << 20),
        cost_estimate=pl.CostEstimate(flops=14 * 10**9, bytes_accessed=12 * 10**6, transcendentals=6 * 10**6),
        name="stack",
    )(*parts, src, jnp.asarray(table), jnp.asarray(edge_table), member)


def crossed(count, stage):
    pairs = []
    for y, z, x, c in np.ndindex(4, 4, 4, 2):
        along_z = c == stage
        to = (y, (z + count) % 4) if along_z else ((y + count) % 4, z)
        pairs.append((((y * 4 + z) * 4 + x) * 2 + c, ((to[0] * 4 + to[1]) * 4 + x) * 2 + c))
    return pairs


def shards(spectra, sources, bin_rows):
    y, z, x, c = (lax.axis_index(a) for a in ("y", "z", "x", "c"))
    chan = y * 4 + z
    chan_dev, win_dev = spectra.shape[:2]
    windows = win_dev * 8
    swap = [(0, 1), (1, 0)]
    slot_rows = bin_rows[:, 0]

    sent = pick(spectra, sources, jnp.transpose(bin_rows, (0, 3, 1, 2)))
    flipped = jnp.transpose(spectra, (2, 1, 0, 3))
    band = np.abs(np.arange(512)[:, None] - 128 - np.arange(256)[None, :]) <= HW
    for stage in range(2):
        got = [lax.ppermute(sent, ("y", "z", "x", "c"), crossed(k, stage)) for k in (1, 3, 2)]
        sent = (sent + got[0]) + (got[1] + got[2])
        if stage == 0:
            sent, flipped = lax.optimization_barrier((sent, flipped))
            mine = whiten(flipped, jnp.asarray(band.astype(bf16)))
    counts = sent[:, 0, 0, F : F + NBINS].astype(f32)
    src = sent[..., :F].reshape(2, 2, 4, 2, F)
    src_mine = lax.dynamic_index_in_dim(src, c, 0, keepdims=False)
    src_other = lax.ppermute(lax.dynamic_index_in_dim(src, 1 - c, 0, keepdims=False), "c", swap)
    src = jnp.transpose(jnp.stack([src_mine, src_other]), (3, 0, 1, 2, 4)).reshape(32, F)
    parts = [mine, lax.ppermute(mine, "c", swap)]

    own_rows = lax.dynamic_slice_in_dim(slot_rows, 2 * c, 2, 0)
    member = jnp.any(own_rows[..., None] == jnp.arange(chan_dev), axis=2).reshape(2, 16, 2, chan_dev)
    member = jnp.transpose(member, (1, 0, 2, 3)).astype(bf16)
    eye = jnp.eye(2, dtype=bf16)
    member = (
        member[:, None, :, :, None, None, :]
        * eye[None, :, None, None, :, None, None]
        * eye[None, None, :, None, None, :, None]
    ).reshape(128, 4 * chan_dev)

    partial = stack_partial(parts, src, member)
    received = lax.all_to_all(partial.reshape(64, 6, 8, HALF), ("y", "z", "x"), 0, 0, tiled=True)
    totals = jnp.sum(received.astype(f32), axis=0).reshape(2, 3, 2, 2, 2, HALF)
    counts = lax.dynamic_slice(counts, (2 * c, 2 * chan), (2, 2))
    traces = (jnp.maximum(counts, 1.0) * windows)[None, None, :, :, None]
    linear, pr, pi = totals[:, 0] * (1.0 / 32.0), totals[:, 1], totals[:, 2]
    stacked = linear / jnp.sqrt(traces) * (pr * pr + pi * pi) / traces
    keep = lax.dynamic_index_in_dim(stacked, c, 0, keepdims=False)
    send = lax.dynamic_index_in_dim(stacked, 1 - c, 0, keepdims=False)
    got = lax.ppermute(send, "c", swap)
    both = jnp.where(c == 0, jnp.stack([keep, got]), jnp.stack([got, keep]))
    out = jnp.transpose(both, (0, 2, 3, 1, 4)).reshape(4, 2, BLOCK)
    return jnp.where(x < 2, out[..., ::-1], out)


def solution(mesh):
    fine = Mesh(mesh.devices.reshape(4, 4, 4, 2), ("y", "z", "x", "c"))
    chan, win = ("y", "z"), ("x", "c")
    in_specs = (P(chan, win, None, None), P(), P(None, chan, None, None))
    return jax.shard_map(
        shards, mesh=fine, in_specs=in_specs, out_specs=P(None, chan, win), check_vma=False
    )
```

```python
import jax
import jax.numpy as jnp
import numpy as np
from jax import lax
from jax.experimental import pallas as pl
from jax.experimental.pallas import tpu as pltpu
from jax.sharding import Mesh, PartitionSpec as P

F = 1024
F0 = 32
NFFT = 8192
HW = 32
NBINS = 32
EPS = 1e-06
FLOOR = 0.1
BLOCK = 512
HALF = 256
PAIRS = 4
bf16 = jnp.bfloat16
f32 = jnp.float32


def lag_tables():
    frequency = F0 + np.arange(F, dtype=np.int64)

    def pair(lags):
        angle = (frequency[:, None] * lags[None, :]) % NFFT * (2.0 * np.pi / NFFT)
        return np.concatenate([np.cos(angle), np.sin(angle)], axis=1).astype(bf16)

    blocks = [
        np.concatenate(
            [pair(b * BLOCK + h * HALF + np.arange(HALF)) for h in range(2)], axis=1
        )
        for b in range(PAIRS)
    ]
    return np.stack(blocks), pair(np.full((128,), 2048))


def smooth_amplitude(re, im):
    amp = jnp.sqrt(re * re + im * im)
    wide = F + 128
    padded = jnp.concatenate([amp, jnp.zeros((amp.shape[0], 128), f32)], axis=1)
    total = padded
    for k in (1, 2, 4, 8, 16, 32):
        total = total + pltpu.roll(total, k, 1)
    total = pltpu.roll(total, wide - HW, 1) + pltpu.roll(padded, HW, 1)
    return total[:, :F] * (1.0 / (2 * HW + 1)) + EPS


def pick_kernel(sources_ref, slots_ref, spectra_ref, out_ref, sem):
    me = lax.axis_index("y") * 4 + lax.axis_index("z")
    for s in range(4):
        owner, row = sources_ref[s] // 48, sources_ref[s] % 48
        copy = pltpu.make_async_copy(spectra_ref.at[row], out_ref.at[s, :, :, pl.ds(0, F)], sem.at[s])

        @pl.when(owner == me)
        def _(copy=copy):
            copy.start()

        @pl.when(owner != me)
        def _(s=s):
            out_ref[s, :, :, :F] = jnp.zeros((4, 2, F), bf16)

        live = (slots_ref[s] >= 0).astype(f32)
        count = live[0] + live[1] + live[2]
        out_ref[s, :, :, F:] = jnp.zeros((4, 2, 128), bf16)
        out_ref[s, 0, :, F : F + NBINS] = jnp.broadcast_to(count, (2, NBINS)).astype(bf16)

    for s in range(4):
        owner, row = sources_ref[s] // 48, sources_ref[s] % 48
        copy = pltpu.make_async_copy(spectra_ref.at[row], out_ref.at[s, :, :, pl.ds(0, F)], sem.at[s])

        @pl.when(owner == me)
        def _(copy=copy):
            copy.wait()


def pick(spectra, sources, slots):
    return pl.pallas_call(
        pick_kernel,
        in_specs=[
            pl.BlockSpec(memory_space=pltpu.SMEM),
            pl.BlockSpec(memory_space=pltpu.VMEM),
            pl.BlockSpec(memory_space=pl.ANY),
        ],
        out_specs=pl.BlockSpec(memory_space=pltpu.VMEM),
        out_shape=jax.ShapeDtypeStruct((4, 4, 2, F + 128), bf16),
        scratch_shapes=[pltpu.SemaphoreType.DMA((4,))],
        name="pick",
    )(sources, slots, spectra)


def whiten_kernel(x_ref, band_ref, o_ref, amp_sc):
    edge = jnp.zeros((384, 128), bf16)
    amp_sc[:, :128] = edge
    amp_sc[:, 128 + F :] = edge
    for w in range(4):
        re = x_ref[0, w].astype(f32)
        im = x_ref[1, w].astype(f32)
        amp = jnp.sqrt(re * re + im * im)
        high = amp.astype(bf16)
        amp_sc[48 * w : 48 * w + 48, 128 : 128 + F] = high
        amp_sc[192 + 48 * w : 192 + 48 * w + 48, 128 : 128 + F] = (amp - high.astype(f32)).astype(bf16)
    for n in range(4):
        lanes = slice(256 * n, 256 * n + 256)
        total = jnp.dot(amp_sc[:, 256 * n : 256 * n + 512], band_ref[...], preferred_element_type=f32)
        total = (total[:192] + total[192:]) * (1.0 / (2 * HW + 1)) + EPS
        inv = 1.0 / total
        for w in range(4):
            part = inv[48 * w : 48 * w + 48]
            o_ref[0, w, :, lanes] = (x_ref[0, w, :, lanes].astype(f32) * part).astype(bf16)
            o_ref[1, w, :, lanes] = (x_ref[1, w, :, lanes].astype(f32) * part).astype(bf16)


def whiten(x, band):
    vmem = pl.BlockSpec(memory_space=pltpu.VMEM)
    return pl.pallas_call(
        whiten_kernel,
        in_specs=[vmem, vmem],
        out_specs=vmem,
        out_shape=jax.ShapeDtypeStruct(x.shape, bf16),
        scratch_shapes=[pltpu.VMEM((384, F + 256), bf16)],
        cost_estimate=pl.CostEstimate(flops=8 * 10**8, bytes_accessed=2 * 10**6, transcendentals=4 * 10**5),
        name="whiten",
    )(x, band)


def stack_kernel(
    mine_ref, other_ref, src_ref, table_ref, edge_table_ref, member_ref, out_ref,
    src_sc, cross_sc, prod_sc, edge_prod_sc, minus_sc, plus_sc, edge_sc, sums_sc, table_sc, table_sem, part_sc, part_sem, out_sc, out_sem,
):
    step_id = pl.program_id(0)
    block = PAIRS - 1 - step_id
    floor2 = (FLOOR * 32.0) ** 2
    slot = step_id % 2

    def fetch(step):
        return pltpu.make_async_copy(table_ref.at[PAIRS - 1 - step], table_sc.at[step % 2], table_sem.at[step % 2])

    def leave(done, sign):
        win = PAIRS - 1 - done if sign else PAIRS + done
        return pltpu.make_async_copy(out_sc.at[:, win], out_ref.at[:, win], out_sem.at[done, sign])

    parts = [
        pltpu.make_async_copy(ref, part_sc.at[i], part_sem.at[i])
        for i, ref in enumerate((mine_ref, other_ref))
    ]

    @pl.when(step_id == 0)
    def _():
        for copy in parts:
            copy.start()
        fetch(0).start()

    @pl.when(step_id < PAIRS - 1)
    def _():
        fetch(step_id + 1).start()

    def unit(re, im):
        inv = lax.rsqrt(jnp.maximum(re * re + im * im, floor2))
        return re * inv, im * inv

    @pl.when(step_id == 0)
    def _():
        re = src_ref[0:16, :].astype(f32)
        im = src_ref[16:32, :].astype(f32)
        inv = 1.0 / smooth_amplitude(re, im)
        src_sc[0] = (re * inv).astype(bf16).astype(f32)
        src_sc[1] = (im * inv).astype(bf16).astype(f32)
        for w in range(8):
            half, wl = divmod(w, 4)
            if wl == 0:
                parts[half].wait()
            for s in range(2):
                row = half * 8 + s * 4 + wl
                ref = part_sc.at[half]
                for g in range(3):
                    rows = slice(16 * g, 16 * g + 16)
                    sr = jnp.broadcast_to(src_sc[0, row : row + 1, :], (16, F))
                    si = jnp.broadcast_to(src_sc[1, row : row + 1, :], (16, F))
                    wr = ref[0, wl, rows, :].astype(f32)
                    wi = ref[1, wl, rows, :].astype(f32)
                    at = w * 48 + 16 * g
                    cross_sc[s, at : at + 16, :] = (wr * sr + wi * si).astype(bf16)
                    cross_sc[s, 384 + at : 384 + at + 16, :] = (wi * sr - wr * si).astype(bf16)
        for s in range(2):
            edge_prod_sc[...] = jnp.dot(cross_sc[s], edge_table_ref[...], preferred_element_type=f32)
            for g in range(6):
                lin = jnp.zeros((8, 128), f32)
                pr, pi = lin, lin
                for w in range(8):
                    at = w * 48 + 8 * g
                    a = edge_prod_sc[at : at + 8, :128]
                    d = edge_prod_sc[at : at + 8, 128:]
                    c = edge_prod_sc[384 + at : 384 + at + 8, :128]
                    b = edge_prod_sc[384 + at : 384 + at + 8, 128:]
                    lin = lin + (a + b)
                    ur, ui = unit(a + b, c - d)
                    pr, pi = pr + ur, pi + ui
                for k, value in enumerate((lin, pr, pi)):
                    edge_sc[k, s, 8 * g : 8 * g + 8, :] = value

    def product(i):
        h, s = divmod(i, 2)
        prod_sc[i % 2] = jnp.dot(
            cross_sc[s], table_sc[slot, :, h * 512 : h * 512 + 512], preferred_element_type=f32
        )

    def epilogue(i):
        h, s = divmod(i, 2)
        slot = i % 2
        for g in range(6):
            for t in range(2):
                zero = jnp.zeros((8, 128), f32)
                sa, sb, pr, pi, mr, mi = (zero,) * 6
                for w in range(8):
                    at = w * 48 + 8 * g
                    lo = slice(128 * t, 128 * t + 128)
                    hi = slice(256 + 128 * t, 256 + 128 * t + 128)
                    a = prod_sc[slot, at : at + 8, lo]
                    d = prod_sc[slot, at : at + 8, hi]
                    c = prod_sc[slot, 384 + at : 384 + at + 8, lo]
                    b = prod_sc[slot, 384 + at : 384 + at + 8, hi]
                    sa, sb = sa + a, sb + b
                    ur, ui = unit(a - b, c + d)
                    pr, pi = pr + ur, pi + ui
                    ur, ui = unit(a + b, c - d)
                    mr, mi = mr + ur, mi + ui
                at = h * 96 + s * 48 + 8 * g
                for k, value in enumerate((sa - sb, pr, pi)):
                    plus_sc[k, at : at + 8, 128 * t : 128 * t + 128] = value
                for k, value in enumerate((sa + sb, mr, mi)):
                    lo = 256 * h + 128 * t
                    minus_sc[k, s, 8 * g : 8 * g + 8, lo : lo + 128] = value

    fetch(step_id).wait()
    product(0)
    for i in range(1, 4):
        product(i)
        epilogue(i - 1)
    epilogue(3)
    last = lax.broadcasted_iota(jnp.int32, (48, 128), 1) == 127
    for k in range(3):
        for s in range(2):
            moved = pltpu.roll(minus_sc[k, s], BLOCK - 1, 1)
            tail = moved[:, 384:]
            new_tail = jnp.where(last, edge_sc[k, s], tail)
            edge_sc[k, s] = tail
            at = s * 48
            sums_sc[1, k, at : at + 48, :] = moved[:, :256].astype(bf16)
            sums_sc[1, k, 96 + at : 96 + at + 48, :128] = moved[:, 256:384].astype(bf16)
            sums_sc[1, k, 96 + at : 96 + at + 48, 128:] = new_tail.astype(bf16)
    for sign in range(2):
        win = PAIRS - 1 - block if sign else PAIRS + block
        for k in range(3):
            sums = sums_sc[1, k] if sign else plus_sc[k].astype(bf16)
            binned = jnp.dot(member_ref[...], sums, preferred_element_type=f32)
            out_sc[:, win, k] = binned.reshape(16, 8, HALF).astype(bf16)
        leave(block, sign).start()

    @pl.when(step_id == PAIRS - 1)
    def _():
        for done in range(PAIRS):
            for sign in range(2):
                leave(done, sign).wait()


def stack_partial(parts, src, member):
    table, edge_table = lag_tables()
    hbm = pl.BlockSpec(memory_space=pl.ANY)
    vmem = pl.BlockSpec(memory_space=pltpu.VMEM)
    return pl.pallas_call(
        stack_kernel,
        grid=(PAIRS,),
        in_specs=[pl.BlockSpec(memory_space=pltpu.HBM)] * 2 + [vmem, hbm, vmem, vmem],
        out_specs=hbm,
        out_shape=jax.ShapeDtypeStruct((16, 8, 3, 8, HALF), bf16),
        scratch_shapes=[
            pltpu.VMEM((2, 16, F), f32),
            pltpu.VMEM((2, 768, F), bf16),
            pltpu.VMEM((2, 768, 512), f32),
            pltpu.VMEM((768, 256), f32),
            pltpu.VMEM((3, 2, 48, BLOCK), f32),
            pltpu.VMEM((3, 192, HALF), f32),
            pltpu.VMEM((3, 2, 48, 128), f32),
            pltpu.VMEM((2, 3, 192, HALF), bf16),
            pltpu.VMEM((2, F, 1024), bf16),
            pltpu.SemaphoreType.DMA((2,)),
            pltpu.VMEM((2, 2, 4, 48, F), bf16),
            pltpu.SemaphoreType.DMA((2,)),
            pltpu.VMEM((16, 8, 3, 8, HALF), bf16),
            pltpu.SemaphoreType.DMA((PAIRS, 2)),
        ],
        compiler_params=pltpu.CompilerParams(vmem_limit_bytes=48 << 20),
        cost_estimate=pl.CostEstimate(flops=14 * 10**9, bytes_accessed=12 * 10**6, transcendentals=6 * 10**6),
        name="stack",
    )(*parts, src, jnp.asarray(table), jnp.asarray(edge_table), member)


def crossed(count, stage):
    pairs = []
    for y, z, x, c in np.ndindex(4, 4, 4, 2):
        along_z = c == stage
        to = (y, (z + count) % 4) if along_z else ((y + count) % 4, z)
        pairs.append((((y * 4 + z) * 4 + x) * 2 + c, ((to[0] * 4 + to[1]) * 4 + x) * 2 + c))
    return pairs


def shards(spectra, sources, bin_rows):
    y, z, x, c = (lax.axis_index(a) for a in ("y", "z", "x", "c"))
    chan = y * 4 + z
    chan_dev, win_dev = spectra.shape[:2]
    windows = win_dev * 8
    swap = [(0, 1), (1, 0)]
    slot_rows = bin_rows[:, 0]

    sent = pick(spectra, sources, jnp.transpose(bin_rows, (0, 3, 1, 2)))
    flipped = jnp.transpose(spectra, (2, 1, 0, 3))
    band = np.abs(np.arange(512)[:, None] - 128 - np.arange(256)[None, :]) <= HW
    for stage in range(2):
        got = [lax.ppermute(sent, ("y", "z", "x", "c"), crossed(k, stage)) for k in (1, 3, 2)]
        sent = (sent + got[0]) + (got[1] + got[2])
        if stage == 0:
            sent, flipped = lax.optimization_barrier((sent, flipped))
            mine = whiten(flipped, jnp.asarray(band.astype(bf16)))
    counts = sent[:, 0, 0, F : F + NBINS].astype(f32)
    src = sent[..., :F].reshape(2, 2, 4, 2, F)
    src_mine = lax.dynamic_index_in_dim(src, c, 0, keepdims=False)
    src_other = lax.ppermute(lax.dynamic_index_in_dim(src, 1 - c, 0, keepdims=False), "c", swap)
    src = jnp.transpose(jnp.stack([src_mine, src_other]), (3, 0, 1, 2, 4)).reshape(32, F)
    parts = [mine, lax.ppermute(mine, "c", swap)]

    own_rows = lax.dynamic_slice_in_dim(slot_rows, 2 * c, 2, 0)
    member = jnp.any(own_rows[..., None] == jnp.arange(chan_dev), axis=2).reshape(2, 16, 2, chan_dev)
    member = jnp.transpose(member, (1, 0, 2, 3)).astype(bf16)
    eye = jnp.eye(2, dtype=bf16)
    member = (
        member[:, None, :, :, None, None, :]
        * eye[None, :, None, None, :, None, None]
        * eye[None, None, :, None, None, :, None]
    ).reshape(128, 4 * chan_dev)

    partial = stack_partial(parts, src, member)
    received = lax.all_to_all(partial.reshape(64, 6, 8, HALF), ("y", "z", "x"), 0, 0, tiled=True)
    totals = jnp.sum(received.astype(f32), axis=0).reshape(2, 3, 2, 2, 2, HALF)
    counts = lax.dynamic_slice(counts, (2 * c, 2 * chan), (2, 2))
    traces = (jnp.maximum(counts, 1.0) * windows)[None, None, :, :, None]
    linear, pr, pi = totals[:, 0] * (1.0 / 32.0), totals[:, 1], totals[:, 2]
    stacked = linear / jnp.sqrt(traces) * (pr * pr + pi * pi) / traces
    keep = lax.dynamic_index_in_dim(stacked, c, 0, keepdims=False)
    send = lax.dynamic_index_in_dim(stacked, 1 - c, 0, keepdims=False)
    got = lax.ppermute(send, "c", swap)
    both = jnp.where(c == 0, jnp.stack([keep, got]), jnp.stack([got, keep]))
    out = jnp.transpose(both, (0, 2, 3, 1, 4)).reshape(4, 2, BLOCK)
    return jnp.where(x < 2, out[..., ::-1], out)


def solution(mesh):
    fine = Mesh(mesh.devices.reshape(4, 4, 4, 2), ("y", "z", "x", "c"))
    chan, win = ("y", "z"), ("x", "c")
    in_specs = (P(chan, win, None, None), P(), P(None, chan, None, None))
    return jax.shard_map(
        shards, mesh=fine, in_specs=in_specs, out_specs=P(None, chan, win), check_vma=False
    )
```

```python
import jax
import jax.numpy as jnp
import numpy as np
from jax import lax
from jax.experimental import pallas as pl
from jax.experimental.pallas import tpu as pltpu
from jax.sharding import Mesh, PartitionSpec as P

F = 1024
F0 = 32
NFFT = 8192
HW = 32
NBINS = 32
EPS = 1e-06
FLOOR = 0.1
BLOCK = 512
HALF = 256
PAIRS = 4
bf16 = jnp.bfloat16
f32 = jnp.float32


def lag_tables():
    frequency = F0 + np.arange(F, dtype=np.int64)

    def pair(lags):
        angle = (frequency[:, None] * lags[None, :]) % NFFT * (2.0 * np.pi / NFFT)
        return np.concatenate([np.cos(angle), np.sin(angle)], axis=1).astype(bf16)

    blocks = [
        np.concatenate(
            [pair(b * BLOCK + h * HALF + np.arange(HALF)) for h in range(2)], axis=1
        )
        for b in range(PAIRS)
    ]
    return np.stack(blocks), pair(np.full((128,), 2048))


def smooth_amplitude(re, im):
    amp = jnp.sqrt(re * re + im * im)
    wide = F + 128
    padded = jnp.concatenate([amp, jnp.zeros((amp.shape[0], 128), f32)], axis=1)
    total = padded
    for k in (1, 2, 4, 8, 16, 32):
        total = total + pltpu.roll(total, k, 1)
    total = pltpu.roll(total, wide - HW, 1) + pltpu.roll(padded, HW, 1)
    return total[:, :F] * (1.0 / (2 * HW + 1)) + EPS


def pick_kernel(sources_ref, slots_ref, spectra_ref, out_ref, sem):
    me = lax.axis_index("y") * 4 + lax.axis_index("z")
    for s in range(4):
        owner, row = sources_ref[s] // 48, sources_ref[s] % 48
        copy = pltpu.make_async_copy(spectra_ref.at[row], out_ref.at[s, :, :, pl.ds(0, F)], sem.at[s])

        @pl.when(owner == me)
        def _(copy=copy):
            copy.start()

        @pl.when(owner != me)
        def _(s=s):
            out_ref[s, :, :, :F] = jnp.zeros((4, 2, F), bf16)

        live = (slots_ref[s] >= 0).astype(f32)
        count = live[0] + live[1] + live[2]
        out_ref[s, :, :, F:] = jnp.zeros((4, 2, 128), bf16)
        out_ref[s, 0, :, F : F + NBINS] = jnp.broadcast_to(count, (2, NBINS)).astype(bf16)

    for s in range(4):
        owner, row = sources_ref[s] // 48, sources_ref[s] % 48
        copy = pltpu.make_async_copy(spectra_ref.at[row], out_ref.at[s, :, :, pl.ds(0, F)], sem.at[s])

        @pl.when(owner == me)
        def _(copy=copy):
            copy.wait()


def pick(spectra, sources, slots):
    return pl.pallas_call(
        pick_kernel,
        in_specs=[
            pl.BlockSpec(memory_space=pltpu.SMEM),
            pl.BlockSpec(memory_space=pltpu.VMEM),
            pl.BlockSpec(memory_space=pl.ANY),
        ],
        out_specs=pl.BlockSpec(memory_space=pltpu.VMEM),
        out_shape=jax.ShapeDtypeStruct((4, 4, 2, F + 128), bf16),
        scratch_shapes=[pltpu.SemaphoreType.DMA((4,))],
        name="pick",
    )(sources, slots, spectra)


def whiten_kernel(x_ref, band_ref, o_ref, amp_sc):
    edge = jnp.zeros((384, 128), bf16)
    amp_sc[:, :128] = edge
    amp_sc[:, 128 + F :] = edge
    for w in range(4):
        re = x_ref[0, w].astype(f32)
        im = x_ref[1, w].astype(f32)
        amp = jnp.sqrt(re * re + im * im)
        high = amp.astype(bf16)
        amp_sc[48 * w : 48 * w + 48, 128 : 128 + F] = high
        amp_sc[192 + 48 * w : 192 + 48 * w + 48, 128 : 128 + F] = (amp - high.astype(f32)).astype(bf16)
    for n in range(4):
        lanes = slice(256 * n, 256 * n + 256)
        total = jnp.dot(amp_sc[:, 256 * n : 256 * n + 512], band_ref[...], preferred_element_type=f32)
        total = (total[:192] + total[192:]) * (1.0 / (2 * HW + 1)) + EPS
        inv = 1.0 / total
        for w in range(4):
            part = inv[48 * w : 48 * w + 48]
            o_ref[0, w, :, lanes] = (x_ref[0, w, :, lanes].astype(f32) * part).astype(bf16)
            o_ref[1, w, :, lanes] = (x_ref[1, w, :, lanes].astype(f32) * part).astype(bf16)


def whiten(x, band):
    vmem = pl.BlockSpec(memory_space=pltpu.VMEM)
    return pl.pallas_call(
        whiten_kernel,
        in_specs=[vmem, vmem],
        out_specs=vmem,
        out_shape=pltpu.VMEM(x.shape, bf16),
        scratch_shapes=[pltpu.VMEM((384, F + 256), bf16)],
        cost_estimate=pl.CostEstimate(flops=8 * 10**8, bytes_accessed=2 * 10**6, transcendentals=4 * 10**5),
        name="whiten",
    )(x, band)


def stack_kernel(
    mine_ref, other_ref, src_ref, table_ref, edge_table_ref, member_ref, out_ref,
    src_sc, cross_sc, prod_sc, edge_prod_sc, minus_sc, plus_sc, edge_sc, sums_sc, table_sc, table_sem, part_sc, part_sem, out_sc, out_sem,
):
    step_id = pl.program_id(0)
    block = PAIRS - 1 - step_id
    floor2 = (FLOOR * 32.0) ** 2
    slot = step_id % 2

    def fetch(step):
        return pltpu.make_async_copy(table_ref.at[PAIRS - 1 - step], table_sc.at[step % 2], table_sem.at[step % 2])

    def leave(done, sign):
        win = PAIRS - 1 - done if sign else PAIRS + done
        return pltpu.make_async_copy(out_sc.at[:, win], out_ref.at[:, win], out_sem.at[done, sign])

    parts = [
        pltpu.make_async_copy(ref, part_sc.at[i], part_sem.at[i])
        for i, ref in enumerate((mine_ref, other_ref))
    ]

    @pl.when(step_id == 0)
    def _():
        for copy in parts:
            copy.start()
        fetch(0).start()

    @pl.when(step_id < PAIRS - 1)
    def _():
        fetch(step_id + 1).start()

    def unit(re, im):
        inv = lax.rsqrt(jnp.maximum(re * re + im * im, floor2))
        return re * inv, im * inv

    @pl.when(step_id == 0)
    def _():
        re = src_ref[0:16, :].astype(f32)
        im = src_ref[16:32, :].astype(f32)
        inv = 1.0 / smooth_amplitude(re, im)
        src_sc[0] = (re * inv).astype(bf16).astype(f32)
        src_sc[1] = (im * inv).astype(bf16).astype(f32)
        for w in range(8):
            half, wl = divmod(w, 4)
            if wl == 0:
                parts[half].wait()
            for s in range(2):
                row = half * 8 + s * 4 + wl
                ref = part_sc.at[half]
                for g in range(3):
                    rows = slice(16 * g, 16 * g + 16)
                    sr = jnp.broadcast_to(src_sc[0, row : row + 1, :], (16, F))
                    si = jnp.broadcast_to(src_sc[1, row : row + 1, :], (16, F))
                    wr = ref[0, wl, rows, :].astype(f32)
                    wi = ref[1, wl, rows, :].astype(f32)
                    at = w * 48 + 16 * g
                    cross_sc[s, at : at + 16, :] = (wr * sr + wi * si).astype(bf16)
                    cross_sc[s, 384 + at : 384 + at + 16, :] = (wi * sr - wr * si).astype(bf16)
        for s in range(2):
            edge_prod_sc[...] = jnp.dot(cross_sc[s], edge_table_ref[...], preferred_element_type=f32)
            for g in range(6):
                lin = jnp.zeros((8, 128), f32)
                pr, pi = lin, lin
                for w in range(8):
                    at = w * 48 + 8 * g
                    a = edge_prod_sc[at : at + 8, :128]
                    d = edge_prod_sc[at : at + 8, 128:]
                    c = edge_prod_sc[384 + at : 384 + at + 8, :128]
                    b = edge_prod_sc[384 + at : 384 + at + 8, 128:]
                    lin = lin + (a + b)
                    ur, ui = unit(a + b, c - d)
                    pr, pi = pr + ur, pi + ui
                for k, value in enumerate((lin, pr, pi)):
                    edge_sc[k, s, 8 * g : 8 * g + 8, :] = value

    def product(i):
        h, s = divmod(i, 2)
        prod_sc[i % 2] = jnp.dot(
            cross_sc[s], table_sc[slot, :, h * 512 : h * 512 + 512], preferred_element_type=f32
        )

    def epilogue(i):
        h, s = divmod(i, 2)
        slot = i % 2
        for g in range(6):
            for t in range(2):
                zero = jnp.zeros((8, 128), f32)
                sa, sb, pr, pi, mr, mi = (zero,) * 6
                for w in range(8):
                    at = w * 48 + 8 * g
                    lo = slice(128 * t, 128 * t + 128)
                    hi = slice(256 + 128 * t, 256 + 128 * t + 128)
                    a = prod_sc[slot, at : at + 8, lo]
                    d = prod_sc[slot, at : at + 8, hi]
                    c = prod_sc[slot, 384 + at : 384 + at + 8, lo]
                    b = prod_sc[slot, 384 + at : 384 + at + 8, hi]
                    sa, sb = sa + a, sb + b
                    ur, ui = unit(a - b, c + d)
                    pr, pi = pr + ur, pi + ui
                    ur, ui = unit(a + b, c - d)
                    mr, mi = mr + ur, mi + ui
                at = h * 96 + s * 48 + 8 * g
                for k, value in enumerate((sa - sb, pr, pi)):
                    plus_sc[k, at : at + 8, 128 * t : 128 * t + 128] = value
                for k, value in enumerate((sa + sb, mr, mi)):
                    lo = 256 * h + 128 * t
                    minus_sc[k, s, 8 * g : 8 * g + 8, lo : lo + 128] = value

    fetch(step_id).wait()
    product(0)
    for i in range(1, 4):
        product(i)
        epilogue(i - 1)
    epilogue(3)
    last = lax.broadcasted_iota(jnp.int32, (48, 128), 1) == 127
    for k in range(3):
        for s in range(2):
            moved = pltpu.roll(minus_sc[k, s], BLOCK - 1, 1)
            tail = moved[:, 384:]
            new_tail = jnp.where(last, edge_sc[k, s], tail)
            edge_sc[k, s] = tail
            at = s * 48
            sums_sc[1, k, at : at + 48, :] = moved[:, :256].astype(bf16)
            sums_sc[1, k, 96 + at : 96 + at + 48, :128] = moved[:, 256:384].astype(bf16)
            sums_sc[1, k, 96 + at : 96 + at + 48, 128:] = new_tail.astype(bf16)
    for sign in range(2):
        win = PAIRS - 1 - block if sign else PAIRS + block
        for k in range(3):
            sums = sums_sc[1, k] if sign else plus_sc[k].astype(bf16)
            binned = jnp.dot(member_ref[...], sums, preferred_element_type=f32)
            out_sc[:, win, k] = binned.reshape(16, 8, HALF).astype(bf16)
        leave(block, sign).start()

    @pl.when(step_id == PAIRS - 1)
    def _():
        for done in range(PAIRS):
            for sign in range(2):
                leave(done, sign).wait()


def stack_partial(parts, src, member):
    table, edge_table = lag_tables()
    hbm = pl.BlockSpec(memory_space=pl.ANY)
    vmem = pl.BlockSpec(memory_space=pltpu.VMEM)
    return pl.pallas_call(
        stack_kernel,
        grid=(PAIRS,),
        in_specs=[hbm, hbm, vmem, hbm, vmem, vmem],
        out_specs=hbm,
        out_shape=jax.ShapeDtypeStruct((16, 8, 3, 8, HALF), bf16),
        scratch_shapes=[
            pltpu.VMEM((2, 16, F), f32),
            pltpu.VMEM((2, 768, F), bf16),
            pltpu.VMEM((2, 768, 512), f32),
            pltpu.VMEM((768, 256), f32),
            pltpu.VMEM((3, 2, 48, BLOCK), f32),
            pltpu.VMEM((3, 192, HALF), f32),
            pltpu.VMEM((3, 2, 48, 128), f32),
            pltpu.VMEM((2, 3, 192, HALF), bf16),
            pltpu.VMEM((2, F, 1024), bf16),
            pltpu.SemaphoreType.DMA((2,)),
            pltpu.VMEM((2, 2, 4, 48, F), bf16),
            pltpu.SemaphoreType.DMA((2,)),
            pltpu.VMEM((16, 8, 3, 8, HALF), bf16),
            pltpu.SemaphoreType.DMA((PAIRS, 2)),
        ],
        compiler_params=pltpu.CompilerParams(vmem_limit_bytes=48 << 20),
        cost_estimate=pl.CostEstimate(flops=14 * 10**9, bytes_accessed=12 * 10**6, transcendentals=6 * 10**6),
        name="stack",
    )(*parts, src, jnp.asarray(table), jnp.asarray(edge_table), member)


def crossed(count, stage):
    pairs = []
    for y, z, x, c in np.ndindex(4, 4, 4, 2):
        along_z = c == stage
        to = (y, (z + count) % 4) if along_z else ((y + count) % 4, z)
        pairs.append((((y * 4 + z) * 4 + x) * 2 + c, ((to[0] * 4 + to[1]) * 4 + x) * 2 + c))
    return pairs


def shards(spectra, sources, bin_rows):
    y, z, x, c = (lax.axis_index(a) for a in ("y", "z", "x", "c"))
    chan = y * 4 + z
    chan_dev, win_dev = spectra.shape[:2]
    windows = win_dev * 8
    swap = [(0, 1), (1, 0)]
    slot_rows = bin_rows[:, 0]

    sent = pick(spectra, sources, jnp.transpose(bin_rows, (0, 3, 1, 2)))
    flipped = jnp.transpose(spectra, (2, 1, 0, 3))
    band = np.abs(np.arange(512)[:, None] - 128 - np.arange(256)[None, :]) <= HW
    for stage in range(2):
        got = [lax.ppermute(sent, ("y", "z", "x", "c"), crossed(k, stage)) for k in (1, 3, 2)]
        sent = (sent + got[0]) + (got[1] + got[2])
        if stage == 0:
            sent, flipped = lax.optimization_barrier((sent, flipped))
            mine = whiten(flipped, jnp.asarray(band.astype(bf16)))
    counts = sent[:, 0, 0, F : F + NBINS].astype(f32)
    src = sent[..., :F].reshape(2, 2, 4, 2, F)
    src_mine = lax.dynamic_index_in_dim(src, c, 0, keepdims=False)
    src_other = lax.ppermute(lax.dynamic_index_in_dim(src, 1 - c, 0, keepdims=False), "c", swap)
    src = jnp.transpose(jnp.stack([src_mine, src_other]), (3, 0, 1, 2, 4)).reshape(32, F)
    parts = [mine, lax.ppermute(mine, "c", swap)]

    own_rows = lax.dynamic_slice_in_dim(slot_rows, 2 * c, 2, 0)
    member = jnp.any(own_rows[..., None] == jnp.arange(chan_dev), axis=2).reshape(2, 16, 2, chan_dev)
    member = jnp.transpose(member, (1, 0, 2, 3)).astype(bf16)
    eye = jnp.eye(2, dtype=bf16)
    member = (
        member[:, None, :, :, None, None, :]
        * eye[None, :, None, None, :, None, None]
        * eye[None, None, :, None, None, :, None]
    ).reshape(128, 4 * chan_dev)

    partial = stack_partial(parts, src, member)
    received = lax.all_to_all(partial.reshape(64, 6, 8, HALF), ("y", "z", "x"), 0, 0, tiled=True)
    totals = jnp.sum(received.astype(f32), axis=0).reshape(2, 3, 2, 2, 2, HALF)
    counts = lax.dynamic_slice(counts, (2 * c, 2 * chan), (2, 2))
    traces = (jnp.maximum(counts, 1.0) * windows)[None, None, :, :, None]
    linear, pr, pi = totals[:, 0] * (1.0 / 32.0), totals[:, 1], totals[:, 2]
    stacked = linear / jnp.sqrt(traces) * (pr * pr + pi * pi) / traces
    keep = lax.dynamic_index_in_dim(stacked, c, 0, keepdims=False)
    send = lax.dynamic_index_in_dim(stacked, 1 - c, 0, keepdims=False)
    got = lax.ppermute(send, "c", swap)
    both = jnp.where(c == 0, jnp.stack([keep, got]), jnp.stack([got, keep]))
    out = jnp.transpose(both, (0, 2, 3, 1, 4)).reshape(4, 2, BLOCK)
    return jnp.where(x < 2, out[..., ::-1], out)


def solution(mesh):
    fine = Mesh(mesh.devices.reshape(4, 4, 4, 2), ("y", "z", "x", "c"))
    chan, win = ("y", "z"), ("x", "c")
    in_specs = (P(chan, win, None, None), P(), P(None, chan, None, None))
    return jax.shard_map(
        shards, mesh=fine, in_specs=in_specs, out_specs=P(None, chan, win), check_vma=False
    )
```
